32 devices in a mesh: layer: 2 (over core), prow: 4 (over z), pcol: 4 (over y, x).
Axes of the slice: x: 2, y: 2, z: 4, core: 2. Of those that a mesh axis runs over, the one named last changes fastest.
Arguments:
- diag_inverse: float32 [2, 3, 2048, 2048], P('layer', None, 'prow', 'pcol'), may hold values from -1 to 1, as said below
- root_inverse: float32 [2048, 2048], P('prow', 'pcol'), may hold values from -1 to 1, as said below
- coupling: float32 [2, 5, 2048, 2048], P('layer', None, 'prow', 'pcol'), may hold values from -0.0625 to 0.0625
- tile_mask: int32 [2, 5, 16, 16], P('layer'), may hold values 0 or 1
- sketch: float32 [2, 3, 2048, 256], P('layer', None, 'prow'), may hold values from -6 to 6
- root_sketch: float32 [2048, 256], P('prow'), may hold values from -6 to 6
Outputs:
- solution: float32 [2, 3, 2048, 256], P('layer', None, 'prow')
- root_solution: float32 [2048, 256], P('prow')
The draws below stay inside these ranges and needn't reach their ends.
Inputs may be any that keep to these rules, and one draw needn't show every extreme that they name: `diag_inverse`: lower triangular. `root_inverse`: lower triangular.
All inputs are finite; a program needn't handle non-finite values. No bound on the sum of `tile_mask` on one device may be relied on, other than what follows from the above.
Results may differ from the reference program's by a relative error of at most 0.0001.
Values sent between devices are 32-bit elements; how exact they have to be, the bound alone decides.
No kernel may reach another device: no remote copies, remote signals or barrier semaphores. Data moves between devices by JAX's collectives and lax.ppermute only.
A program may use at most 64 MiB of HBM per device.

```python
import math
import jax
import jax.numpy as jnp
from jax import lax

S = 2048
K = 256
TILE = 128
LAYERS = 2


def lower_factor(key, count):
    row_grid = lax.broadcasted_iota(jnp.int32, (S, S), 0)
    col_grid = lax.broadcasted_iota(jnp.int32, (S, S), 1)
    below = (row_grid > col_grid).astype(jnp.float32)
    noise = jax.random.normal(key, (count, S, S), jnp.float32)
    return noise * below * (0.5 / math.sqrt(S)) + jnp.eye(S, dtype=jnp.float32)


def draw_diag_inverse(key, part):
    return lower_factor(jax.random.fold_in(key, 11), LAYERS * 3).reshape(LAYERS, 3, S, S)


def draw_root_inverse(key, part):
    return lower_factor(jax.random.fold_in(key, 23), 1)[0]


def plant(result, key, least, largest):
    longest = result.shape.index(max(result.shape))
    spots = []
    for shift in (0, 1):
        where = [jax.random.randint(jax.random.fold_in(key, axis), (), 0, length) for axis, length in enumerate(result.shape)]
        where[longest] = (where[longest] + shift) % result.shape[longest]
        spots.append(tuple(where))
    return result.at[spots[0]].set(least).at[spots[1]].set(largest)


def levels(stream_key, extent, cuts, smallest, top_value):
    factor_of = 1.0
    for dim, shards_of in cuts:
        steps = jax.random.uniform(jax.random.fold_in(jax.random.fold_in(stream_key, 6), dim), (shards_of,), jnp.float32, smallest / len(cuts), top_value / len(cuts))
        factor_of = factor_of * jnp.repeat(jnp.exp(steps), extent[dim] // shards_of).reshape((-1,) + (1,) * (len(extent) - 1 - dim))
    return factor_of


def scatter_about(own_key, shape, width, bound, shards=(), held_as=jnp.bfloat16):
    drawn = width * jax.random.normal(own_key, shape, jnp.float32)
    if shards:
        drawn = drawn * levels(own_key, shape, shards, -0.22, 0.18)
    return jnp.clip(drawn, -bound, bound).astype(held_as)


def setup_inputs(seed: int = 0) -> dict:
    key_list = jax.random.split(jax.random.key(seed), 7)
    return {
        "diag_inverse": draw_diag_inverse(jax.random.fold_in(key_list[6], 71), 0),
        "root_inverse": draw_root_inverse(jax.random.fold_in(key_list[6], 71), 0),
        "coupling": scatter_about(key_list[2], (LAYERS, 5, S, S), (4 * S) ** -0.5, 0.0625, ((0, 2), (2, 4), (3, 4)), jnp.float32),
        "tile_mask": plant((jax.random.randint(key_list[3], (LAYERS, 5, S // TILE, S // TILE), 0, 2) < 1).astype(jnp.int32), jax.random.fold_in(key_list[3], 1), 0, 1),
        "sketch": scatter_about(key_list[4], (LAYERS, 3, S, K), 1.0, 6.0, ((0, 2), (2, 4)), jnp.float32),
        "root_sketch": scatter_about(key_list[5], (S, K), 1.0, 6.0, ((0, 4),), jnp.float32),
    }


def forward_product(matrix, vector):
    return jnp.einsum("...ij,...jk->...ik", matrix, vector, precision=lax.Precision.HIGHEST)


def transpose_product(matrix, vector):
    return jnp.einsum("...ij,...ik->...jk", matrix, vector, precision=lax.Precision.HIGHEST)


def reference(diag_inverse, root_inverse, coupling, tile_mask, sketch, root_sketch):
    expanded = jnp.repeat(jnp.repeat(tile_mask, TILE, axis=2), TILE, axis=3).astype(jnp.float32)
    blocks = coupling * expanded
    leaves = forward_product(diag_inverse[:, :2], sketch[:, :2])
    mid_rhs = sketch[:, 2] - forward_product(blocks[:, 0], leaves[:, 0]) - forward_product(blocks[:, 1], leaves[:, 1])
    middle = forward_product(diag_inverse[:, 2], mid_rhs)
    update = forward_product(blocks[:, 2], leaves[:, 0]) + forward_product(blocks[:, 3], leaves[:, 1]) + forward_product(blocks[:, 4], middle)
    update = jnp.sum(update, axis=0)
    root_forward = forward_product(root_inverse, root_sketch - update)
    root_solution = transpose_product(root_inverse, root_forward)
    spread_root = jnp.broadcast_to(root_solution, (LAYERS, S, K))
    mid_back = middle - transpose_product(blocks[:, 4], spread_root)
    mid_solution = transpose_product(diag_inverse[:, 2], mid_back)
    leaf_back = leaves - transpose_product(blocks[:, 0:2], jnp.stack([mid_solution, mid_solution], axis=1))
    leaf_back = leaf_back - transpose_product(blocks[:, 2:4], jnp.stack([spread_root, spread_root], axis=1))
    leaf_solution = transpose_product(diag_inverse[:, :2], leaf_back)
    solution = jnp.concatenate([leaf_solution, mid_solution[:, None]], axis=1)
    return solution, root_solution
```

```python
import jax
import jax.numpy as jnp
from jax import lax
from jax.sharding import PartitionSpec as P

TILE = 128
GRID = ("prow", "pcol")


def dot(matrix, vector):
    return lax.dot_general(
        matrix, vector, (((1,), (0,)), ((), ())), precision=lax.Precision.HIGH
    )


def dot_t(matrix, vector):
    return lax.dot_general(
        matrix, vector, (((0,), (0,)), ((), ())), precision=lax.Precision.HIGH
    )


def send(value, target):
    rows, cols = lax.axis_size("prow"), lax.axis_size("pcol")
    pairs = []
    for i in range(rows):
        for j in range(cols):
            a, b = target(i, j)
            pairs.append((i * cols + j, a * cols + b))
    if all(s == d for s, d in pairs):
        return value
    return lax.ppermute(value, GRID, pairs)


def swap_layers(value):
    return lax.ppermute(value, "layer", [(0, 1), (1, 0)])


def split(value, count):
    size = value.shape[0] // count
    return [value[k * size : (k + 1) * size] for k in range(count)]


def total(pieces):
    result = pieces[0]
    for piece in pieces[1:]:
        result = result + piece
    return result


def reduce_chunks(partial):
    cols = lax.axis_size("pcol")
    pieces = split(partial, cols)
    return total([send(pieces[q], lambda i, j: (i, (j + q) % cols)) for q in range(cols)])


def gather_rows(chunk):
    cols = lax.axis_size("pcol")
    return jnp.concatenate(
        [send(chunk, lambda i, j: (i, (j - q) % cols)) for q in range(cols)], axis=0
    )


def gather_columns(chunk):
    rows, cols = lax.axis_size("prow"), lax.axis_size("pcol")
    ratio = cols // rows
    return jnp.concatenate(
        [
            send(chunk, lambda i, c: ((c % rows - i - q) % rows, i * ratio + c // rows))
            for q in range(rows)
        ],
        axis=0,
    )


def reduce_columns(partial):
    rows, cols = lax.axis_size("prow"), lax.axis_size("pcol")
    ratio = cols // rows
    pieces = split(partial, rows)
    moved = []
    for q in range(rows):
        near = send(
            pieces[q],
            lambda i, j: (i, j % ratio * rows + (i + j // ratio + q) % rows),
        )
        moved.append(send(near, lambda i, c: ((c % rows - i - q) % rows, c)))
    return total(moved)


def rotate(value, start, axis):
    doubled = jnp.concatenate([value, value], axis=axis)
    return lax.dynamic_slice_in_dim(doubled, start, value.shape[axis], axis)


def per_device(diag_inverse, root_inverse, coupling, tile_mask, sketch, root_sketch):
    rows, cols = lax.axis_size("prow"), lax.axis_size("pcol")
    row_index, col_index = lax.axis_index("prow"), lax.axis_index("pcol")
    layer = lax.axis_index("layer")
    ratio = cols // rows
    rows_here, cols_here = root_inverse.shape
    size = rows_here // cols
    width = sketch.shape[3]
    half = width // 2
    row_turn = col_index * size
    col_turn = (row_index + col_index // ratio) % rows * size

    def own(value):
        return lax.dynamic_slice_in_dim(value, col_index * size, size, value.ndim - 2)

    row_tiles = (row_index * rows_here + (row_turn + lax.iota(jnp.int32, rows_here)) % rows_here) // TILE
    col_tiles = (col_index * cols_here + (col_turn + lax.iota(jnp.int32, cols_here)) % cols_here) // TILE
    tiles = tile_mask.shape[2]
    row_pick = (row_tiles[:, None] == lax.iota(jnp.int32, tiles)[None]).astype(jnp.float32)
    col_pick = (lax.iota(jnp.int32, tiles)[:, None] == col_tiles[None]).astype(jnp.float32)

    def turned(matrix):
        return rotate(rotate(matrix, row_turn, 0), col_turn, 1)

    inverse = [turned(diag_inverse[0, n]) for n in range(3)]
    root = turned(root_inverse)
    blocks = []
    for n in range(5):
        mask = row_pick @ tile_mask[0, n].astype(jnp.float32) @ col_pick
        blocks.append(turned(coupling[0, n]) * mask)

    rhs = own(sketch[0])
    root_rhs = own(root_sketch)

    leaves, fed = [], []
    for a in range(2):
        leaves.append(reduce_chunks(dot(inverse[a], gather_columns(rhs[a]))))
        fed.append(gather_columns(leaves[a]))
    mid_part = dot(blocks[0], fed[0]) + dot(blocks[1], fed[1])
    mid_rhs = rhs[2] - reduce_chunks(mid_part)
    root_part = dot(blocks[2], fed[0]) + dot(blocks[3], fed[1])
    middle = reduce_chunks(dot(inverse[2], gather_columns(mid_rhs)))
    root_part = root_part + dot(blocks[4], gather_columns(middle))

    other = swap_layers(lax.dynamic_slice_in_dim(root_part, (1 - layer) * half, half, 1))
    mine = lax.dynamic_slice_in_dim(root_part, layer * half, half, 1) + other
    root_mine = lax.dynamic_slice_in_dim(root_rhs, layer * half, half, 1)
    root_in = gather_columns(root_mine - reduce_chunks(mine))
    root_forward = gather_rows(reduce_chunks(dot(root, root_in)))
    root_half = gather_rows(reduce_columns(dot_t(root, root_forward)))
    other_half = swap_layers(root_half)
    first = layer == 0
    root_rows = jnp.concatenate(
        [jnp.where(first, root_half, other_half), jnp.where(first, other_half, root_half)], axis=1
    )

    mid_back = middle - reduce_columns(dot_t(blocks[4], root_rows))
    mid_solution = reduce_columns(dot_t(inverse[2], gather_rows(mid_back)))
    mid_rows = gather_rows(mid_solution)
    answers = []
    for a in range(2):
        terms = dot_t(blocks[2 + a], root_rows) + dot_t(blocks[a], mid_rows)
        leaf_back = leaves[a] - reduce_columns(terms)
        leaf_chunk = reduce_columns(dot_t(inverse[a], gather_rows(leaf_back)))
        answers.append(gather_rows(leaf_chunk))
    back = rows_here - row_turn
    solution = jnp.stack([rotate(v, back, 0) for v in answers + [mid_rows]])[None]
    return solution, rotate(root_rows, back, 0)


def solution(mesh):
    in_specs = (
        P("layer", None, "prow", "pcol"),
        P("prow", "pcol"),
        P("layer", None, "prow", "pcol"),
        P("layer", None, None, None),
        P("layer", None, "prow", None),
        P("prow", None),
    )
    out_specs = (P("layer", None, "prow", None), P("prow", None))
    return jax.shard_map(
        per_device, mesh=mesh, in_specs=in_specs, out_specs=out_specs, check_vma=False
    )
```

```python
import jax
import jax.numpy as jnp
from jax import lax
from jax.sharding import PartitionSpec as P

TILE = 128


def broadcast(block, axis, owner):
    block = jnp.where(lax.axis_index(axis) == owner, block, jnp.zeros_like(block))
    return lax.psum(block, axis)


def forward_product(matrix, vector):
    return jnp.einsum("nij,njk->nik", matrix, vector, precision=lax.Precision.HIGHEST)


def transpose_product(matrix, vector):
    return jnp.einsum("nij,nik->njk", matrix, vector, precision=lax.Precision.HIGHEST)


def column_panel(vector):
    group_ratio = lax.axis_size("pcol") // lax.axis_size("prow")
    col_index = lax.axis_index("pcol")
    received = broadcast(vector, "prow", col_index // group_ratio)
    col_width = vector.shape[1] // group_ratio
    return lax.dynamic_slice_in_dim(received, col_index % group_ratio * col_width, col_width, 1)


def column_total(partial_value):
    return lax.psum(partial_value, "pcol")


def regroup(column_rows):
    group_ratio = lax.axis_size("pcol") // lax.axis_size("prow")
    row_index = lax.axis_index("prow")
    col_width = column_rows.shape[1]
    complete = lax.all_gather(column_rows, "pcol", axis=1, tiled=True)
    return lax.dynamic_slice_in_dim(
        complete, row_index * (col_width * group_ratio), col_width * group_ratio, 1
    )


def row_total(partial_value):
    return regroup(lax.psum(partial_value, "prow"))


def local_mask(tile_mask, rows_here, cols_here):
    row_tiles = (lax.axis_index("prow") * rows_here + lax.iota(jnp.int32, rows_here)) // TILE
    col_tiles = (lax.axis_index("pcol") * cols_here + lax.iota(jnp.int32, cols_here)) // TILE
    table = jnp.take(tile_mask[0], row_tiles, axis=1)
    table = jnp.take(table, col_tiles, axis=2)
    return table.astype(jnp.float32)


def per_device_any(diag_inverse, root_inverse, coupling, tile_mask, sketch, root_sketch):
    layer_inverse = diag_inverse[0]
    rows_here = coupling.shape[2]
    cols_here = coupling.shape[3]
    blocks = coupling[0] * local_mask(tile_mask, rows_here, cols_here)
    rhs_local = sketch[0]
    leaves = column_total(forward_product(layer_inverse[0:2], column_panel(rhs_local[0:2])))
    fed_leaves = column_panel(leaves)
    mid_part = forward_product(blocks[0:2], fed_leaves)
    root_part = forward_product(blocks[2:4], fed_leaves)
    mid_rhs = rhs_local[2] - column_total(mid_part[0] + mid_part[1])
    middle = column_total(forward_product(layer_inverse[2:3], column_panel(mid_rhs[None])))[0]
    upper_part = forward_product(blocks[4:5], column_panel(middle[None]))[0]
    update = lax.psum(root_part[0] + root_part[1] + upper_part, ("layer", "pcol"))
    root_forward = column_total(
        forward_product(root_inverse[None], column_panel((root_sketch - update)[None]))
    )[0]
    root_solution = row_total(transpose_product(root_inverse[None], root_forward[None]))[0]
    spread_root = jnp.broadcast_to(root_solution, (3,) + root_solution.shape)
    back_terms = row_total(transpose_product(blocks[2:5], spread_root))
    mid_back = middle - back_terms[2]
    mid_solution = row_total(transpose_product(layer_inverse[2:3], mid_back[None]))[0]
    spread_mid = jnp.broadcast_to(mid_solution, (2,) + mid_solution.shape)
    leaf_terms = row_total(transpose_product(blocks[0:2], spread_mid))
    leaf_back = leaves - leaf_terms - back_terms[0:2]
    leaf_solution = row_total(transpose_product(layer_inverse[0:2], leaf_back))
    solution = jnp.concatenate([leaf_solution, mid_solution[None]], axis=0)[None]
    return (solution, root_solution)

AXES = ("layer", "prow", "pcol")


def dot(matrix, vector):
    return lax.dot_general(
        matrix, vector, (((1,), (0,)), ((), ())), precision=lax.Precision.HIGH
    )


def dot_t(matrix, vector):
    return lax.dot_general(
        matrix, vector, (((0,), (0,)), ((), ())), precision=lax.Precision.HIGH
    )


def move(value, target):
    pairs = []
    for c in range(2):
        for i in range(4):
            for y in range(2):
                for x in range(2):
                    to = target(c, i, y, x)
                    if to is not None:
                        a, b, d, e = to
                        pairs.append((((c * 4 + i) * 2 + y) * 2 + x, ((a * 4 + b) * 2 + d) * 2 + e))
    return lax.ppermute(value, AXES, pairs)


def swap_cores(value):
    return lax.ppermute(value, "layer", [(0, 1), (1, 0)])


def swap_x(value):
    return move(value, lambda c, i, y, x: (c, i, y, 1 - x))


def swap_y(value):
    return move(value, lambda c, i, y, x: (c, i, 1 - y, x))


def to_layer_chip(value):
    moved = move(value, lambda c, i, y, x: (y, i, c, x) if c != y else None)
    return jnp.where(lax.axis_index("layer") == lax.axis_index("pcol") // 2, value, moved)


def after(value, earlier):
    return value if earlier is None else lax.optimization_barrier((value, earlier))[0]


def per_device_square(diag_inverse, root_inverse, coupling, tile_mask, sketch, root_sketch):
    core, z = lax.axis_index("layer"), lax.axis_index("prow")
    y, x = lax.axis_index("pcol") // 2, lax.axis_index("pcol") % 2
    rows_here, cols_here = root_inverse.shape
    half = sketch.shape[3] // 2
    owner = core == z // 2
    straight = z % 2 == x
    root_owner = z == 2 * core + y

    def columns(value, which):
        return lax.dynamic_slice_in_dim(value, which * half, half, value.ndim - 1)

    def along_z(value, sends, distances=(1, 2, 3)):
        return [
            move(value, lambda c, i, y, x: (c, i ^ k, y, x) if sends(c, i, i ^ k, y, x) else None)
            for k in distances
        ]

    rhs = jnp.where(core == y, sketch[0], swap_cores(sketch[0]))
    root_rhs = columns(root_sketch, x)
    first_fed = []
    for a in range(2):
        sent = along_z(rhs[a], lambda c, i, to, y, x: i == 2 * c + x)
        first_fed.append(jnp.where(z == 2 * core + x, rhs[a], sent[0] + sent[1] + sent[2]))

    tiles = tile_mask.shape[2]
    row_tiles = (z * rows_here + lax.iota(jnp.int32, rows_here)) // TILE
    col_tiles = ((2 * y + x) * cols_here + lax.iota(jnp.int32, cols_here)) // TILE
    row_pick = (row_tiles[:, None] == lax.iota(jnp.int32, tiles)[None]).astype(jnp.float32)
    col_pick = (lax.iota(jnp.int32, tiles)[:, None] == col_tiles[None]).astype(jnp.float32)

    def blocks(first, last):
        rows = jnp.einsum("rt,ntu->nru", row_pick, tile_mask[0, first:last].astype(jnp.float32))
        return coupling[0, first:last] * jnp.einsum("nru,uc->nrc", rows, col_pick)

    near = {"d01": to_layer_chip(diag_inverse[0, 0:2])}
    near["c01"] = to_layer_chip(after(blocks(0, 2), first_fed[0]))
    far = {}

    def gather(value):
        one, two, three = along_z(value, lambda c, i, to, y, x: c == i // 2)
        even, odd = jnp.where(owner, value, two), jnp.where(owner, one, three)
        return jnp.where(straight, even, odd), jnp.where(straight, odd, even)

    def product(name, n, panels):
        return dot(near[name][n], panels[0]) + dot(far[name][n], panels[1])

    def both_cores(part):
        return part + swap_cores(part)

    def spread(value):
        return jnp.where(owner, value, swap_cores(value))

    leaves, fed = [], []
    for a in range(2):
        part = dot(near["d01"][a], first_fed[a])
        leaves.append(both_cores(columns(part, x) + swap_x(columns(part, 1 - x))))
    near["d2"] = to_layer_chip(after(diag_inverse[0, 2:3], leaves[0]))
    near["c4"] = to_layer_chip(after(blocks(4, 5), leaves[0]))
    far["c01"] = swap_x(after(near["c01"], leaves[1]))
    far["d2"] = swap_x(after(near["d2"], far["c01"]))
    far["c4"] = swap_x(after(near["c4"], far["d2"]))
    for a in range(2):
        fed.append(gather(leaves[a]))
    fed[0] = after(fed[0], far["c01"])
    near["c23"] = to_layer_chip(after(blocks(2, 4), fed[0][0]))
    far["d01"] = swap_x(after(near["d01"], far["c4"]))
    root = move(
        after(root_inverse, fed[1][0]),
        lambda c, i, y, x: None if c == y == x else (y, i, x, c),
    )
    root = jnp.where((core == y) & (y == x), root_inverse, root)
    mid_rhs = columns(rhs[2], x) - both_cores(product("c01", 0, fed[0]) + product("c01", 1, fed[1]))
    root_part = sum(dot(near["c23"][a], fed[a][0]) for a in range(2))
    root_part = root_part + swap_x(sum(dot(near["c23"][a], swap_x(fed[a][1])) for a in range(2)))
    middle = both_cores(product("d2", 0, gather(mid_rhs)))
    root_part = root_part + product("c4", 0, gather(middle))

    def plane_total(part):
        part = both_cores(part)
        return part + swap_y(part)

    root_in = root_rhs - plane_total(root_part)
    sent = along_z(root_in, lambda c, i, to, y, x: i == 2 * c + y)
    root_fed = jnp.where(root_owner, root_in, sent[0] + sent[1] + sent[2])
    root_forward = plane_total(dot(root, root_fed))
    root_back = dot_t(root, root_forward)
    sent = along_z(root_back, lambda c, i, to, y, x: to == 2 * c + y)
    root_back = spread(root_back + sent[0] + sent[1] + sent[2])
    root_rows = after(jnp.where(y == z % 2, root_back, swap_y(root_back)), far["d01"])

    def terms(name, n, value):
        return dot_t(near[name][n], value), dot_t(far[name][n], value)

    def reduce(near_part, far_part):
        even = jnp.where(straight, near_part, far_part)
        odd = jnp.where(straight, far_part, near_part)
        (one,) = along_z(odd, lambda c, i, to, y, x: c == i // 2, (1,))
        (two,) = along_z(even, lambda c, i, to, y, x: c != i // 2, (2,))
        (three,) = along_z(odd, lambda c, i, to, y, x: c != i // 2, (3,))
        return even + one + two + three

    def full_width(value, other=None):
        other = swap_x(value) if other is None else other
        first = x == 0
        return jnp.concatenate(
            [jnp.where(first, value, other), jnp.where(first, other, value)], axis=-1
        )

    root_other = swap_x(root_rows)
    root_terms = [
        (dot_t(near["c23"][a], root_rows), swap_x(dot_t(near["c23"][a], root_other)))
        for a in range(2)
    ]
    mid_back = spread(middle - reduce(*terms("c4", 0, root_rows)))
    mid_rows = spread(reduce(*terms("d2", 0, mid_back)))
    answers = []
    for a in range(2):
        from_root, from_mid = root_terms[a], terms("c01", a, mid_rows)
        leaf_back = leaves[a] - reduce(from_root[0] + from_mid[0], from_root[1] + from_mid[1])
        leaf_rows = spread(reduce(*terms("d01", a, spread(leaf_back))))
        answers.append(full_width(to_layer_chip(leaf_rows)))
    answers.append(full_width(to_layer_chip(mid_rows)))
    return jnp.stack(answers)[None], full_width(root_rows, root_other)


def solution(mesh):
    square = dict(mesh.shape) == {"layer": 2, "prow": 4, "pcol": 4}
    per_device = per_device_square if square else per_device_any
    in_specs = (
        P("layer", None, "prow", "pcol"),
        P("prow", "pcol"),
        P("layer", None, "prow", "pcol"),
        P("layer", None, None, None),
        P("layer", None, "prow", None),
        P("prow", None),
    )
    out_specs = (P("layer", None, "prow", None), P("prow", None))
    return jax.shard_map(
        per_device, mesh=mesh, in_specs=in_specs, out_specs=out_specs, check_vma=False
    )
```

```python
import jax
import jax.numpy as jnp
from jax import lax
from jax.sharding import PartitionSpec as P

TILE = 128


def broadcast(block, axis, owner):
    block = jnp.where(lax.axis_index(axis) == owner, block, jnp.zeros_like(block))
    return lax.psum(block, axis)


def forward_product(matrix, vector):
    return jnp.einsum("nij,njk->nik", matrix, vector, precision=lax.Precision.HIGHEST)


def transpose_product(matrix, vector):
    return jnp.einsum("nij,nik->njk", matrix, vector, precision=lax.Precision.HIGHEST)


def column_panel(vector):
    group_ratio = lax.axis_size("pcol") // lax.axis_size("prow")
    col_index = lax.axis_index("pcol")
    received = broadcast(vector, "prow", col_index // group_ratio)
    col_width = vector.shape[1] // group_ratio
    return lax.dynamic_slice_in_dim(received, col_index % group_ratio * col_width, col_width, 1)


def column_total(partial_value):
    return lax.psum(partial_value, "pcol")


def regroup(column_rows):
    group_ratio = lax.axis_size("pcol") // lax.axis_size("prow")
    row_index = lax.axis_index("prow")
    col_width = column_rows.shape[1]
    complete = lax.all_gather(column_rows, "pcol", axis=1, tiled=True)
    return lax.dynamic_slice_in_dim(
        complete, row_index * (col_width * group_ratio), col_width * group_ratio, 1
    )


def row_total(partial_value):
    return regroup(lax.psum(partial_value, "prow"))


def local_mask(tile_mask, rows_here, cols_here):
    row_tiles = (lax.axis_index("prow") * rows_here + lax.iota(jnp.int32, rows_here)) // TILE
    col_tiles = (lax.axis_index("pcol") * cols_here + lax.iota(jnp.int32, cols_here)) // TILE
    table = jnp.take(tile_mask[0], row_tiles, axis=1)
    table = jnp.take(table, col_tiles, axis=2)
    return table.astype(jnp.float32)


def per_device_any(diag_inverse, root_inverse, coupling, tile_mask, sketch, root_sketch):
    layer_inverse = diag_inverse[0]
    rows_here = coupling.shape[2]
    cols_here = coupling.shape[3]
    blocks = coupling[0] * local_mask(tile_mask, rows_here, cols_here)
    rhs_local = sketch[0]
    leaves = column_total(forward_product(layer_inverse[0:2], column_panel(rhs_local[0:2])))
    fed_leaves = column_panel(leaves)
    mid_part = forward_product(blocks[0:2], fed_leaves)
    root_part = forward_product(blocks[2:4], fed_leaves)
    mid_rhs = rhs_local[2] - column_total(mid_part[0] + mid_part[1])
    middle = column_total(forward_product(layer_inverse[2:3], column_panel(mid_rhs[None])))[0]
    upper_part = forward_product(blocks[4:5], column_panel(middle[None]))[0]
    update = lax.psum(root_part[0] + root_part[1] + upper_part, ("layer", "pcol"))
    root_forward = column_total(
        forward_product(root_inverse[None], column_panel((root_sketch - update)[None]))
    )[0]
    root_solution = row_total(transpose_product(root_inverse[None], root_forward[None]))[0]
    spread_root = jnp.broadcast_to(root_solution, (3,) + root_solution.shape)
    back_terms = row_total(transpose_product(blocks[2:5], spread_root))
    mid_back = middle - back_terms[2]
    mid_solution = row_total(transpose_product(layer_inverse[2:3], mid_back[None]))[0]
    spread_mid = jnp.broadcast_to(mid_solution, (2,) + mid_solution.shape)
    leaf_terms = row_total(transpose_product(blocks[0:2], spread_mid))
    leaf_back = leaves - leaf_terms - back_terms[0:2]
    leaf_solution = row_total(transpose_product(layer_inverse[0:2], leaf_back))
    solution = jnp.concatenate([leaf_solution, mid_solution[None]], axis=0)[None]
    return (solution, root_solution)

GRID = ("prow", "pcol")
SIDE = 4


def dot(matrices, vectors):
    return jnp.einsum("nij,njk->nik", matrices, vectors, precision=lax.Precision.HIGH)


def dot_t(matrices, vectors):
    return jnp.einsum("nij,nik->njk", matrices, vectors, precision=lax.Precision.HIGH)


def send(value, target):
    pairs = []
    for i in range(SIDE):
        for j in range(SIDE):
            a, b = target(i, j)
            if (a, b) != (i, j):
                pairs.append((i * SIDE + j, a * SIDE + b))
    return lax.ppermute(value, GRID, pairs)


def swap_layers(value):
    return lax.ppermute(value, "layer", [(0, 1), (1, 0)])


def pick(values, index):
    low = jnp.where(index % 2 == 0, values[0], values[1])
    high = jnp.where(index % 2 == 0, values[2], values[3])
    return jnp.where(index // 2 == 0, low, high)


def per_device_square(diag_inverse, root_inverse, coupling, tile_mask, sketch, root_sketch):
    i, j = lax.axis_index("prow"), lax.axis_index("pcol")
    layer = lax.axis_index("layer")
    rows_here, cols_here = root_inverse.shape
    size = rows_here // SIDE
    half = sketch.shape[3] // 2

    def chunk(value, index):
        return lax.dynamic_slice_in_dim(value, index * size, size, value.ndim - 2)

    def ordered(value, turn, axis):
        parts = [
            lax.dynamic_slice_in_dim(value, (turn ^ k) * size, size, axis) for k in range(SIDE)
        ]
        return jnp.concatenate(parts, axis=axis)

    def arranged(matrices):
        return ordered(ordered(matrices, j, 1), i, 2)

    def reduce_rows(partial):
        parts = [partial[:, k * size : (k + 1) * size] for k in range(SIDE)]
        moved = [send(parts[k], lambda a, b: (a, b ^ k)) for k in range(1, SIDE)]
        return parts[0] + moved[0] + moved[1] + moved[2]

    def gather_parts(value):
        return [value] + [send(value, lambda a, b: (a, b ^ k)) for k in range(1, SIDE)]

    def gather_rows(value):
        return jnp.concatenate(gather_parts(value), axis=1)

    def gather_columns(value):
        parts = [send(value, lambda a, b: (b ^ k, a)) for k in range(SIDE)]
        parts[0] = jnp.where(i == j, value, parts[0])
        return jnp.concatenate(parts, axis=1)

    def reduce_columns(partial):
        parts = [chunk(partial, i ^ j ^ k) for k in range(SIDE)]
        near = [parts[0]] + [send(parts[k], lambda a, b: (a, b ^ k)) for k in range(1, SIDE)]
        parts = [pick(near, i ^ j ^ k) for k in range(SIDE)]
        moved = [send(parts[k], lambda a, b: (a ^ k, b)) for k in range(1, SIDE)]
        return parts[0] + moved[0] + moved[1] + moved[2]

    def natural(parts):
        return jnp.concatenate([pick(parts, j ^ k) for k in range(SIDE)], axis=1)

    def columns(value, which):
        return lax.dynamic_slice_in_dim(value, which * half, half, value.ndim - 1)

    order = lax.iota(jnp.int32, rows_here)
    row_tiles = (i * rows_here + ((order // size) ^ j) * size + order % size) // TILE
    col_tiles = (j * cols_here + ((order // size) ^ i) * size + order % size) // TILE
    tiles = lax.iota(jnp.int32, tile_mask.shape[2])
    row_pick = (row_tiles[:, None] == tiles[None]).astype(jnp.float32)
    col_pick = (tiles[:, None] == col_tiles[None]).astype(jnp.float32)

    def blocks(first, last):
        rows = jnp.einsum("rt,ntu->nru", row_pick, tile_mask[0, first:last].astype(jnp.float32))
        return arranged(coupling[0, first:last]) * jnp.einsum("nru,uc->nrc", rows, col_pick)

    rhs = chunk(sketch[0], j)
    root_rhs = chunk(root_sketch, j)

    lower = arranged(diag_inverse[0, 0:2])
    leaves = reduce_rows(dot(lower, gather_columns(rhs[0:2])))
    fed = gather_columns(leaves)
    to_mid, to_root, mid_root = blocks(0, 2), blocks(2, 4), blocks(4, 5)
    upper = arranged(diag_inverse[0, 2:3])
    root = arranged(root_inverse[None])
    mid_part = jnp.sum(dot(to_mid, fed), axis=0, keepdims=True)
    mid_rhs = rhs[2:3] - reduce_rows(mid_part)
    root_part = jnp.sum(dot(to_root, fed), axis=0, keepdims=True)
    middle = reduce_rows(dot(upper, gather_columns(mid_rhs)))
    root_part = root_part + dot(mid_root, gather_columns(middle))

    mine = columns(root_part, layer) + swap_layers(columns(root_part, 1 - layer))
    root_in = columns(root_rhs, layer)[None] - reduce_rows(mine)
    root_forward = gather_rows(reduce_rows(dot(root, gather_columns(root_in))))
    root_half = gather_rows(reduce_columns(dot_t(root, root_forward)))
    other_half = swap_layers(root_half)
    first = layer == 0
    root_rows = jnp.concatenate(
        [jnp.where(first, root_half, other_half), jnp.where(first, other_half, root_half)], axis=2
    )

    def both(value):
        return jnp.broadcast_to(value, (2,) + value.shape[1:])

    from_root = dot_t(to_root, both(root_rows))
    mid_back = middle - reduce_columns(dot_t(mid_root, root_rows))
    mid_parts = gather_parts(reduce_columns(dot_t(upper, gather_rows(mid_back))))
    mid_rows = jnp.concatenate(mid_parts, axis=1)
    leaf_back = leaves - reduce_columns(from_root + dot_t(to_mid, both(mid_rows)))
    leaf_parts = gather_parts(reduce_columns(dot_t(lower, gather_rows(leaf_back))))
    solved = jnp.concatenate([natural(leaf_parts), natural(mid_parts)], axis=0)
    root_parts = [root_rows[:, k * size : (k + 1) * size] for k in range(SIDE)]
    return solved[None], natural(root_parts)[0]


def solution(mesh):
    square = dict(mesh.shape) == {"layer": 2, "prow": SIDE, "pcol": SIDE}
    per_device = per_device_square if square else per_device_any
    in_specs = (
        P("layer", None, "prow", "pcol"),
        P("prow", "pcol"),
        P("layer", None, "prow", "pcol"),
        P("layer", None, None, None),
        P("layer", None, "prow", None),
        P("prow", None),
    )
    out_specs = (P("layer", None, "prow", None), P("prow", None))
    return jax.shard_map(
        per_device, mesh=mesh, in_specs=in_specs, out_specs=out_specs, check_vma=False
    )
```

```python
import jax
import jax.numpy as jnp
from jax import lax
from jax.sharding import PartitionSpec as P

TILE = 128


def broadcast(block, axis, owner):
    block = jnp.where(lax.axis_index(axis) == owner, block, jnp.zeros_like(block))
    return lax.psum(block, axis)


def forward_product(matrix, vector):
    return jnp.einsum("nij,njk->nik", matrix, vector, precision=lax.Precision.HIGHEST)


def transpose_product(matrix, vector):
    return jnp.einsum("nij,nik->njk", matrix, vector, precision=lax.Precision.HIGHEST)


def column_panel(vector):
    group_ratio = lax.axis_size("pcol") // lax.axis_size("prow")
    col_index = lax.axis_index("pcol")
    received = broadcast(vector, "prow", col_index // group_ratio)
    col_width = vector.shape[1] // group_ratio
    return lax.dynamic_slice_in_dim(received, col_index % group_ratio * col_width, col_width, 1)


def column_total(partial_value):
    return lax.psum(partial_value, "pcol")


def regroup(column_rows):
    group_ratio = lax.axis_size("pcol") // lax.axis_size("prow")
    row_index = lax.axis_index("prow")
    col_width = column_rows.shape[1]
    complete = lax.all_gather(column_rows, "pcol", axis=1, tiled=True)
    return lax.dynamic_slice_in_dim(
        complete, row_index * (col_width * group_ratio), col_width * group_ratio, 1
    )


def row_total(partial_value):
    return regroup(lax.psum(partial_value, "prow"))


def local_mask(tile_mask, rows_here, cols_here):
    row_tiles = (lax.axis_index("prow") * rows_here + lax.iota(jnp.int32, rows_here)) // TILE
    col_tiles = (lax.axis_index("pcol") * cols_here + lax.iota(jnp.int32, cols_here)) // TILE
    table = jnp.take(tile_mask[0], row_tiles, axis=1)
    table = jnp.take(table, col_tiles, axis=2)
    return table.astype(jnp.float32)


def per_device_any(diag_inverse, root_inverse, coupling, tile_mask, sketch, root_sketch):
    layer_inverse = diag_inverse[0]
    rows_here = coupling.shape[2]
    cols_here = coupling.shape[3]
    blocks = coupling[0] * local_mask(tile_mask, rows_here, cols_here)
    rhs_local = sketch[0]
    leaves = column_total(forward_product(layer_inverse[0:2], column_panel(rhs_local[0:2])))
    fed_leaves = column_panel(leaves)
    mid_part = forward_product(blocks[0:2], fed_leaves)
    root_part = forward_product(blocks[2:4], fed_leaves)
    mid_rhs = rhs_local[2] - column_total(mid_part[0] + mid_part[1])
    middle = column_total(forward_product(layer_inverse[2:3], column_panel(mid_rhs[None])))[0]
    upper_part = forward_product(blocks[4:5], column_panel(middle[None]))[0]
    update = lax.psum(root_part[0] + root_part[1] + upper_part, ("layer", "pcol"))
    root_forward = column_total(
        forward_product(root_inverse[None], column_panel((root_sketch - update)[None]))
    )[0]
    root_solution = row_total(transpose_product(root_inverse[None], root_forward[None]))[0]
    spread_root = jnp.broadcast_to(root_solution, (3,) + root_solution.shape)
    back_terms = row_total(transpose_product(blocks[2:5], spread_root))
    mid_back = middle - back_terms[2]
    mid_solution = row_total(transpose_product(layer_inverse[2:3], mid_back[None]))[0]
    spread_mid = jnp.broadcast_to(mid_solution, (2,) + mid_solution.shape)
    leaf_terms = row_total(transpose_product(blocks[0:2], spread_mid))
    leaf_back = leaves - leaf_terms - back_terms[0:2]
    leaf_solution = row_total(transpose_product(layer_inverse[0:2], leaf_back))
    solution = jnp.concatenate([leaf_solution, mid_solution[None]], axis=0)[None]
    return (solution, root_solution)

GRID = ("prow", "pcol")
SIDE = 4


def dot(matrices, vectors):
    return jnp.einsum("nij,njk->nik", matrices, vectors, precision=lax.Precision.HIGH)


def dot_t(matrices, vectors):
    return jnp.einsum("nij,nik->njk", matrices, vectors, precision=lax.Precision.HIGH)


def send(value, target):
    pairs = []
    for i in range(SIDE):
        for j in range(SIDE):
            a, b = target(i, j)
            if (a, b) != (i, j):
                pairs.append((i * SIDE + j, a * SIDE + b))
    return lax.ppermute(value, GRID, pairs)


def swap_layers(value):
    return lax.ppermute(value, "layer", [(0, 1), (1, 0)])


def pick(values, index):
    low = jnp.where(index % 2 == 0, values[0], values[1])
    high = jnp.where(index % 2 == 0, values[2], values[3])
    return jnp.where(index // 2 == 0, low, high)


def per_device_square(diag_inverse, root_inverse, coupling, tile_mask, sketch, root_sketch):
    i, j = lax.axis_index("prow"), lax.axis_index("pcol")
    layer = lax.axis_index("layer")
    rows_here, cols_here = root_inverse.shape
    size = rows_here // SIDE
    half = sketch.shape[3] // 2

    def chunk(value, index):
        return lax.dynamic_slice_in_dim(value, index * size, size, value.ndim - 2)

    def ordered(value, turn, axis):
        parts = [
            lax.dynamic_slice_in_dim(value, (turn ^ k) * size, size, axis) for k in range(SIDE)
        ]
        return jnp.concatenate(parts, axis=axis)

    def arranged(matrices):
        return ordered(ordered(matrices, j, 1), i, 2)

    def reduce_rows(partial):
        parts = [partial[:, k * size : (k + 1) * size] for k in range(SIDE)]
        moved = [send(parts[k], lambda a, b: (a, b ^ k)) for k in range(1, SIDE)]
        return parts[0] + moved[0] + moved[1] + moved[2]

    def gather_parts(value):
        return [value] + [send(value, lambda a, b: (a, b ^ k)) for k in range(1, SIDE)]

    def gather_rows(value):
        return jnp.concatenate(gather_parts(value), axis=1)

    def gather_columns(value):
        parts = [send(value, lambda a, b: (b ^ k, a)) for k in range(SIDE)]
        parts[0] = jnp.where(i == j, value, parts[0])
        return jnp.concatenate(parts, axis=1)

    def reduce_columns(partial):
        parts = [chunk(partial, i ^ j ^ k) for k in range(SIDE)]
        near = [parts[0]] + [send(parts[k], lambda a, b: (a, b ^ k)) for k in range(1, SIDE)]
        parts = [pick(near, i ^ j ^ k) for k in range(SIDE)]
        moved = [send(parts[k], lambda a, b: (a ^ k, b)) for k in range(1, SIDE)]
        return parts[0] + moved[0] + moved[1] + moved[2]

    def natural(parts):
        return jnp.concatenate([pick(parts, j ^ k) for k in range(SIDE)], axis=1)

    def columns(value, which):
        return lax.dynamic_slice_in_dim(value, which * half, half, value.ndim - 1)

    order = lax.iota(jnp.int32, rows_here)
    row_tiles = (i * rows_here + ((order // size) ^ j) * size + order % size) // TILE
    col_tiles = (j * cols_here + ((order // size) ^ i) * size + order % size) // TILE
    tiles = lax.iota(jnp.int32, tile_mask.shape[2])
    row_pick = (row_tiles[:, None] == tiles[None]).astype(jnp.float32)
    col_pick = (tiles[:, None] == col_tiles[None]).astype(jnp.float32)

    def blocks(first, last):
        rows = jnp.einsum("rt,ntu->nru", row_pick, tile_mask[0, first:last].astype(jnp.float32))
        return arranged(coupling[0, first:last]) * jnp.einsum("nru,uc->nrc", rows, col_pick)

    rhs = chunk(sketch[0], j)
    root_rhs = chunk(root_sketch, j)

    lower = arranged(diag_inverse[0, 0:2])
    first = gather_columns(rhs[0:2])
    leaves, fed = [], []
    for a in range(2):
        leaves.append(reduce_rows(dot(lower[a : a + 1], first[a : a + 1])))
        fed.append(gather_columns(leaves[a]))
    to_mid, to_root, mid_root = blocks(0, 2), blocks(2, 4), blocks(4, 5)
    upper = arranged(diag_inverse[0, 2:3])
    root = arranged(root_inverse[None])
    mid_part = dot(to_mid[0:1], fed[0]) + dot(to_mid[1:2], fed[1])
    mid_rhs = rhs[2:3] - reduce_rows(mid_part)
    root_part = dot(to_root[0:1], fed[0]) + dot(to_root[1:2], fed[1])
    middle = reduce_rows(dot(upper, gather_columns(mid_rhs)))
    root_part = root_part + dot(mid_root, gather_columns(middle))

    mine = columns(root_part, layer) + swap_layers(columns(root_part, 1 - layer))
    root_in = columns(root_rhs, layer)[None] - reduce_rows(mine)
    root_forward = gather_rows(reduce_rows(dot(root, gather_columns(root_in))))
    root_half = gather_rows(reduce_columns(dot_t(root, root_forward)))
    other_half = swap_layers(root_half)
    first = layer == 0
    root_rows = jnp.concatenate(
        [jnp.where(first, root_half, other_half), jnp.where(first, other_half, root_half)], axis=2
    )

    def both(value):
        return jnp.broadcast_to(value, (2,) + value.shape[1:])

    from_root = dot_t(to_root, both(root_rows))
    mid_back = middle - reduce_columns(dot_t(mid_root, root_rows))
    mid_parts = gather_parts(reduce_columns(dot_t(upper, gather_rows(mid_back))))
    mid_rows = jnp.concatenate(mid_parts, axis=1)
    solved = []
    for a in range(2):
        leaf = slice(a, a + 1)
        terms = from_root[leaf] + dot_t(to_mid[leaf], mid_rows)
        leaf_back = leaves[a] - reduce_columns(terms)
        solved.append(natural(gather_parts(reduce_columns(dot_t(lower[leaf], gather_rows(leaf_back))))))
    solved = jnp.concatenate(solved + [natural(mid_parts)], axis=0)
    root_parts = [root_rows[:, k * size : (k + 1) * size] for k in range(SIDE)]
    return solved[None], natural(root_parts)[0]


def solution(mesh):
    square = dict(mesh.shape) == {"layer": 2, "prow": SIDE, "pcol": SIDE}
    per_device = per_device_square if square else per_device_any
    in_specs = (
        P("layer", None, "prow", "pcol"),
        P("prow", "pcol"),
        P("layer", None, "prow", "pcol"),
        P("layer", None, None, None),
        P("layer", None, "prow", None),
        P("prow", None),
    )
    out_specs = (P("layer", None, "prow", None), P("prow", None))
    return jax.shard_map(
        per_device, mesh=mesh, in_specs=in_specs, out_specs=out_specs, check_vma=False
    )
```

```python
import jax
import jax.numpy as jnp
from jax import lax
from jax.sharding import PartitionSpec as P

TILE = 128


def broadcast(block, axis, owner):
    block = jnp.where(lax.axis_index(axis) == owner, block, jnp.zeros_like(block))
    return lax.psum(block, axis)


def forward_product(matrix, vector):
    return jnp.einsum("nij,njk->nik", matrix, vector, precision=lax.Precision.HIGHEST)


def transpose_product(matrix, vector):
    return jnp.einsum("nij,nik->njk", matrix, vector, precision=lax.Precision.HIGHEST)


def column_panel(vector):
    group_ratio = lax.axis_size("pcol") // lax.axis_size("prow")
    col_index = lax.axis_index("pcol")
    received = broadcast(vector, "prow", col_index // group_ratio)
    col_width = vector.shape[1] // group_ratio
    return lax.dynamic_slice_in_dim(received, col_index % group_ratio * col_width, col_width, 1)


def column_total(partial_value):
    return lax.psum(partial_value, "pcol")


def regroup(column_rows):
    group_ratio = lax.axis_size("pcol") // lax.axis_size("prow")
    row_index = lax.axis_index("prow")
    col_width = column_rows.shape[1]
    complete = lax.all_gather(column_rows, "pcol", axis=1, tiled=True)
    return lax.dynamic_slice_in_dim(
        complete, row_index * (col_width * group_ratio), col_width * group_ratio, 1
    )


def row_total(partial_value):
    return regroup(lax.psum(partial_value, "prow"))


def local_mask(tile_mask, rows_here, cols_here):
    row_tiles = (lax.axis_index("prow") * rows_here + lax.iota(jnp.int32, rows_here)) // TILE
    col_tiles = (lax.axis_index("pcol") * cols_here + lax.iota(jnp.int32, cols_here)) // TILE
    table = jnp.take(tile_mask[0], row_tiles, axis=1)
    table = jnp.take(table, col_tiles, axis=2)
    return table.astype(jnp.float32)


def per_device_any(diag_inverse, root_inverse, coupling, tile_mask, sketch, root_sketch):
    layer_inverse = diag_inverse[0]
    rows_here = coupling.shape[2]
    cols_here = coupling.shape[3]
    blocks = coupling[0] * local_mask(tile_mask, rows_here, cols_here)
    rhs_local = sketch[0]
    leaves = column_total(forward_product(layer_inverse[0:2], column_panel(rhs_local[0:2])))
    fed_leaves = column_panel(leaves)
    mid_part = forward_product(blocks[0:2], fed_leaves)
    root_part = forward_product(blocks[2:4], fed_leaves)
    mid_rhs = rhs_local[2] - column_total(mid_part[0] + mid_part[1])
    middle = column_total(forward_product(layer_inverse[2:3], column_panel(mid_rhs[None])))[0]
    upper_part = forward_product(blocks[4:5], column_panel(middle[None]))[0]
    update = lax.psum(root_part[0] + root_part[1] + upper_part, ("layer", "pcol"))
    root_forward = column_total(
        forward_product(root_inverse[None], column_panel((root_sketch - update)[None]))
    )[0]
    root_solution = row_total(transpose_product(root_inverse[None], root_forward[None]))[0]
    spread_root = jnp.broadcast_to(root_solution, (3,) + root_solution.shape)
    back_terms = row_total(transpose_product(blocks[2:5], spread_root))
    mid_back = middle - back_terms[2]
    mid_solution = row_total(transpose_product(layer_inverse[2:3], mid_back[None]))[0]
    spread_mid = jnp.broadcast_to(mid_solution, (2,) + mid_solution.shape)
    leaf_terms = row_total(transpose_product(blocks[0:2], spread_mid))
    leaf_back = leaves - leaf_terms - back_terms[0:2]
    leaf_solution = row_total(transpose_product(layer_inverse[0:2], leaf_back))
    solution = jnp.concatenate([leaf_solution, mid_solution[None]], axis=0)[None]
    return (solution, root_solution)

GRID = ("prow", "pcol")
SIDE = 4


def dot(matrices, vectors):
    return jnp.einsum("nij,njk->nik", matrices, vectors, precision=lax.Precision.HIGH)


def dot_t(matrices, vectors):
    return jnp.einsum("nij,nik->njk", matrices, vectors, precision=lax.Precision.HIGH)


def send(value, target):
    pairs = []
    for i in range(SIDE):
        for j in range(SIDE):
            a, b = target(i, j)
            if (a, b) != (i, j):
                pairs.append((i * SIDE + j, a * SIDE + b))
    return lax.ppermute(value, GRID, pairs)


def swap_layers(value):
    return lax.ppermute(value, "layer", [(0, 1), (1, 0)])


def pick(values, index):
    low = jnp.where(index % 2 == 0, values[0], values[1])
    high = jnp.where(index % 2 == 0, values[2], values[3])
    return jnp.where(index // 2 == 0, low, high)


def per_device_square(diag_inverse, root_inverse, coupling, tile_mask, sketch, root_sketch):
    i, j = lax.axis_index("prow"), lax.axis_index("pcol")
    layer = lax.axis_index("layer")
    rows_here, cols_here = root_inverse.shape
    size = rows_here // SIDE
    half = sketch.shape[3] // 2

    def chunk(value, index):
        return lax.dynamic_slice_in_dim(value, index * size, size, value.ndim - 2)

    def natural(parts, turn):
        return jnp.concatenate([pick(parts, turn ^ k) for k in range(SIDE)], axis=1)

    def reduce_rows(partial):
        moved = [send(chunk(partial, j ^ k), lambda a, b: (a, b ^ k)) for k in range(1, SIDE)]
        return chunk(partial, j) + moved[0] + moved[1] + moved[2]

    def gather_rows(value):
        parts = [send(value, lambda a, b: (a, b ^ k)) for k in range(1, SIDE)]
        return natural([value] + parts, j)

    def gather_columns(value):
        parts = [send(value, lambda a, b: (b ^ k, a)) for k in range(SIDE)]
        parts[0] = jnp.where(i == j, value, parts[0])
        return natural(parts, i)

    def reduce_columns(partial):
        near = [chunk(partial, j)] + [
            send(chunk(partial, j ^ k), lambda a, b: (a, b ^ k)) for k in range(1, SIDE)
        ]
        parts = [pick(near, i ^ j ^ k) for k in range(SIDE)]
        moved = [send(parts[k], lambda a, b: (a ^ k, b)) for k in range(1, SIDE)]
        return parts[0] + moved[0] + moved[1] + moved[2]

    def columns(value, which):
        return lax.dynamic_slice_in_dim(value, which * half, half, value.ndim - 1)

    row_tiles = (i * rows_here + lax.iota(jnp.int32, rows_here)) // TILE
    col_tiles = (j * cols_here + lax.iota(jnp.int32, cols_here)) // TILE
    tiles = lax.iota(jnp.int32, tile_mask.shape[2])
    row_pick = (row_tiles[:, None] == tiles[None]).astype(jnp.float32)
    col_pick = (tiles[:, None] == col_tiles[None]).astype(jnp.float32)

    def blocks(first, last):
        rows = jnp.einsum("rt,ntu->nru", row_pick, tile_mask[0, first:last].astype(jnp.float32))
        return coupling[0, first:last] * jnp.einsum("nru,uc->nrc", rows, col_pick)

    rhs = chunk(sketch[0], j)
    root_rhs = chunk(root_sketch, j)

    lower = diag_inverse[0, 0:2]
    first = gather_columns(rhs[0:2])
    leaves, fed = [], []
    for a in range(2):
        leaves.append(reduce_rows(dot(lower[a : a + 1], first[a : a + 1])))
        fed.append(gather_columns(leaves[a]))
    to_mid, to_root, mid_root = blocks(0, 2), blocks(2, 4), blocks(4, 5)
    upper = diag_inverse[0, 2:3]
    root = root_inverse[None]
    mid_part = dot(to_mid[0:1], fed[0]) + dot(to_mid[1:2], fed[1])
    mid_rhs = rhs[2:3] - reduce_rows(mid_part)
    root_part = dot(to_root[0:1], fed[0]) + dot(to_root[1:2], fed[1])
    middle = reduce_rows(dot(upper, gather_columns(mid_rhs)))
    root_part = root_part + dot(mid_root, gather_columns(middle))

    mine = columns(root_part, layer) + swap_layers(columns(root_part, 1 - layer))
    root_in = columns(root_rhs, layer)[None] - reduce_rows(mine)
    root_forward = gather_rows(reduce_rows(dot(root, gather_columns(root_in))))
    root_half = gather_rows(reduce_columns(dot_t(root, root_forward)))
    other_half = swap_layers(root_half)
    first = layer == 0
    root_rows = jnp.concatenate(
        [jnp.where(first, root_half, other_half), jnp.where(first, other_half, root_half)], axis=2
    )

    def both(value):
        return jnp.broadcast_to(value, (2,) + value.shape[1:])

    from_root = dot_t(to_root, both(root_rows))
    mid_back = middle - reduce_columns(dot_t(mid_root, root_rows))
    mid_rows = gather_rows(reduce_columns(dot_t(upper, gather_rows(mid_back))))
    solved = []
    for a in range(2):
        leaf = slice(a, a + 1)
        terms = from_root[leaf] + dot_t(to_mid[leaf], mid_rows)
        leaf_back = leaves[a] - reduce_columns(terms)
        solved.append(gather_rows(reduce_columns(dot_t(lower[leaf], gather_rows(leaf_back)))))
    solved = jnp.concatenate(solved + [mid_rows], axis=0)
    return solved[None], root_rows[0]


def solution(mesh):
    square = dict(mesh.shape) == {"layer": 2, "prow": SIDE, "pcol": SIDE}
    per_device = per_device_square if square else per_device_any
    in_specs = (
        P("layer", None, "prow", "pcol"),
        P("prow", "pcol"),
        P("layer", None, "prow", "pcol"),
        P("layer", None, None, None),
        P("layer", None, "prow", None),
        P("prow", None),
    )
    out_specs = (P("layer", None, "prow", None), P("prow", None))
    return jax.shard_map(
        per_device, mesh=mesh, in_specs=in_specs, out_specs=out_specs, check_vma=False
    )
```

```python
import jax
import jax.numpy as jnp
from jax import lax
from jax.sharding import PartitionSpec as P

TILE = 128


def broadcast(block, axis, owner):
    block = jnp.where(lax.axis_index(axis) == owner, block, jnp.zeros_like(block))
    return lax.psum(block, axis)


def forward_product(matrix, vector):
    return jnp.einsum("nij,njk->nik", matrix, vector, precision=lax.Precision.HIGHEST)


def transpose_product(matrix, vector):
    return jnp.einsum("nij,nik->njk", matrix, vector, precision=lax.Precision.HIGHEST)


def column_panel(vector):
    group_ratio = lax.axis_size("pcol") // lax.axis_size("prow")
    col_index = lax.axis_index("pcol")
    received = broadcast(vector, "prow", col_index // group_ratio)
    col_width = vector.shape[1] // group_ratio
    return lax.dynamic_slice_in_dim(received, col_index % group_ratio * col_width, col_width, 1)


def column_total(partial_value):
    return lax.psum(partial_value, "pcol")


def regroup(column_rows):
    group_ratio = lax.axis_size("pcol") // lax.axis_size("prow")
    row_index = lax.axis_index("prow")
    col_width = column_rows.shape[1]
    complete = lax.all_gather(column_rows, "pcol", axis=1, tiled=True)
    return lax.dynamic_slice_in_dim(
        complete, row_index * (col_width * group_ratio), col_width * group_ratio, 1
    )


def row_total(partial_value):
    return regroup(lax.psum(partial_value, "prow"))


def local_mask(tile_mask, rows_here, cols_here):
    row_tiles = (lax.axis_index("prow") * rows_here + lax.iota(jnp.int32, rows_here)) // TILE
    col_tiles = (lax.axis_index("pcol") * cols_here + lax.iota(jnp.int32, cols_here)) // TILE
    table = jnp.take(tile_mask[0], row_tiles, axis=1)
    table = jnp.take(table, col_tiles, axis=2)
    return table.astype(jnp.float32)


def per_device_any(diag_inverse, root_inverse, coupling, tile_mask, sketch, root_sketch):
    layer_inverse = diag_inverse[0]
    rows_here = coupling.shape[2]
    cols_here = coupling.shape[3]
    blocks = coupling[0] * local_mask(tile_mask, rows_here, cols_here)
    rhs_local = sketch[0]
    leaves = column_total(forward_product(layer_inverse[0:2], column_panel(rhs_local[0:2])))
    fed_leaves = column_panel(leaves)
    mid_part = forward_product(blocks[0:2], fed_leaves)
    root_part = forward_product(blocks[2:4], fed_leaves)
    mid_rhs = rhs_local[2] - column_total(mid_part[0] + mid_part[1])
    middle = column_total(forward_product(layer_inverse[2:3], column_panel(mid_rhs[None])))[0]
    upper_part = forward_product(blocks[4:5], column_panel(middle[None]))[0]
    update = lax.psum(root_part[0] + root_part[1] + upper_part, ("layer", "pcol"))
    root_forward = column_total(
        forward_product(root_inverse[None], column_panel((root_sketch - update)[None]))
    )[0]
    root_solution = row_total(transpose_product(root_inverse[None], root_forward[None]))[0]
    spread_root = jnp.broadcast_to(root_solution, (3,) + root_solution.shape)
    back_terms = row_total(transpose_product(blocks[2:5], spread_root))
    mid_back = middle - back_terms[2]
    mid_solution = row_total(transpose_product(layer_inverse[2:3], mid_back[None]))[0]
    spread_mid = jnp.broadcast_to(mid_solution, (2,) + mid_solution.shape)
    leaf_terms = row_total(transpose_product(blocks[0:2], spread_mid))
    leaf_back = leaves - leaf_terms - back_terms[0:2]
    leaf_solution = row_total(transpose_product(layer_inverse[0:2], leaf_back))
    solution = jnp.concatenate([leaf_solution, mid_solution[None]], axis=0)[None]
    return (solution, root_solution)

GRID = ("prow", "pcol")
SIDE = 4


def dot(matrices, vectors):
    return jnp.einsum("nij,njk->nik", matrices, vectors, precision=lax.Precision.HIGH)


def dot_t(matrices, vectors):
    return jnp.einsum("nij,nik->njk", matrices, vectors, precision=lax.Precision.HIGH)


def send(value, target):
    pairs = []
    for i in range(SIDE):
        for j in range(SIDE):
            a, b = target(i, j)
            if (a, b) != (i, j):
                pairs.append((i * SIDE + j, a * SIDE + b))
    return lax.ppermute(value, GRID, pairs)


def swap_layers(value):
    return lax.ppermute(value, "layer", [(0, 1), (1, 0)])


def pick(values, index):
    low = jnp.where(index % 2 == 0, values[0], values[1])
    high = jnp.where(index % 2 == 0, values[2], values[3])
    return jnp.where(index // 2 == 0, low, high)


def per_device_square(diag_inverse, root_inverse, coupling, tile_mask, sketch, root_sketch):
    i, j = lax.axis_index("prow"), lax.axis_index("pcol")
    layer = lax.axis_index("layer")
    rows_here, cols_here = root_inverse.shape
    size = rows_here // SIDE
    half = sketch.shape[3] // 2

    def chunk(value, index):
        return lax.dynamic_slice_in_dim(value, index * size, size, value.ndim - 2)

    def natural(parts, turn):
        return jnp.concatenate([pick(parts, turn ^ k) for k in range(SIDE)], axis=1)

    def reduce_rows(partial):
        moved = [send(chunk(partial, j ^ k), lambda a, b: (a, b ^ k)) for k in (3, 2, 1)]
        return chunk(partial, j) + moved[0] + moved[1] + moved[2]

    def gather_rows(value):
        parts = [send(value, lambda a, b: (a, b ^ k)) for k in range(1, SIDE)]
        return natural([value] + parts, j)

    def gather_columns(value):
        parts = [send(value, lambda a, b: (b ^ k, a)) for k in range(SIDE)]
        parts[0] = jnp.where(i == j, value, parts[0])
        return natural(parts, i)

    def reduce_columns(partial):
        near = [chunk(partial, j)] + [
            send(chunk(partial, j ^ k), lambda a, b: (a, b ^ k)) for k in range(1, SIDE)
        ]
        parts = [pick(near, i ^ j ^ k) for k in range(SIDE)]
        moved = [send(parts[k], lambda a, b: (a ^ k, b)) for k in (2, 3, 1)]
        return parts[0] + moved[0] + moved[1] + moved[2]

    def columns(value, which):
        return lax.dynamic_slice_in_dim(value, which * half, half, value.ndim - 1)

    row_tiles = (i * rows_here + lax.iota(jnp.int32, rows_here)) // TILE
    col_tiles = (j * cols_here + lax.iota(jnp.int32, cols_here)) // TILE
    tiles = lax.iota(jnp.int32, tile_mask.shape[2])
    row_pick = (row_tiles[:, None] == tiles[None]).astype(jnp.float32)
    col_pick = (tiles[:, None] == col_tiles[None]).astype(jnp.float32)

    def blocks(first, last):
        rows = jnp.einsum("rt,ntu->nru", row_pick, tile_mask[0, first:last].astype(jnp.float32))
        return coupling[0, first:last] * jnp.einsum("nru,uc->nrc", rows, col_pick)

    rhs = chunk(sketch[0], j)
    root_rhs = chunk(root_sketch, j)

    lower = diag_inverse[0, 0:2]
    first = gather_columns(rhs[0:2])
    leaves, fed = [], []
    for a in range(2):
        leaves.append(reduce_rows(dot(lower[a : a + 1], first[a : a + 1])))
        fed.append(gather_columns(leaves[a]))
    to_mid, to_root, mid_root = blocks(0, 2), blocks(2, 4), blocks(4, 5)
    upper = diag_inverse[0, 2:3]
    root = root_inverse[None]
    mid_part = dot(to_mid[0:1], fed[0]) + dot(to_mid[1:2], fed[1])
    mid_rhs = rhs[2:3] - reduce_rows(mid_part)
    root_part = dot(to_root[0:1], fed[0]) + dot(to_root[1:2], fed[1])
    middle = reduce_rows(dot(upper, gather_columns(mid_rhs)))
    root_part = root_part + dot(mid_root, gather_columns(middle))

    mine = columns(root_part, layer) + swap_layers(columns(root_part, 1 - layer))
    root_in = columns(root_rhs, layer)[None] - reduce_rows(mine)
    root_forward = dot(root, gather_columns(root_in))
    root_forward = root_forward + send(root_forward, lambda a, b: (a, b ^ 1))
    root_forward = root_forward + send(root_forward, lambda a, b: (a, b ^ 2))
    root_half = gather_rows(reduce_columns(dot_t(root, root_forward)))
    other_half = swap_layers(root_half)
    first = layer == 0
    root_rows = jnp.concatenate(
        [jnp.where(first, root_half, other_half), jnp.where(first, other_half, root_half)], axis=2
    )

    def both(value):
        return jnp.broadcast_to(value, (2,) + value.shape[1:])

    from_root = dot_t(to_root, both(root_rows))
    mid_back = middle - reduce_columns(dot_t(mid_root, root_rows))
    mid_rows = gather_rows(reduce_columns(dot_t(upper, gather_rows(mid_back))))
    solved = []
    for a in range(2):
        leaf = slice(a, a + 1)
        terms = from_root[leaf] + dot_t(to_mid[leaf], mid_rows)
        leaf_back = leaves[a] - reduce_columns(terms)
        solved.append(gather_rows(reduce_columns(dot_t(lower[leaf], gather_rows(leaf_back)))))
    solved = jnp.concatenate(solved + [mid_rows], axis=0)
    return solved[None], root_rows[0]


def solution(mesh):
    square = dict(mesh.shape) == {"layer": 2, "prow": SIDE, "pcol": SIDE}
    per_device = per_device_square if square else per_device_any
    in_specs = (
        P("layer", None, "prow", "pcol"),
        P("prow", "pcol"),
        P("layer", None, "prow", "pcol"),
        P("layer", None, None, None),
        P("layer", None, "prow", None),
        P("prow", None),
    )
    out_specs = (P("layer", None, "prow", None), P("prow", None))
    return jax.shard_map(
        per_device, mesh=mesh, in_specs=in_specs, out_specs=out_specs, check_vma=False
    )
```

```python
import jax
import jax.numpy as jnp
from jax import lax
from jax.sharding import PartitionSpec as P

TILE = 128


def broadcast(block, axis, owner):
    block = jnp.where(lax.axis_index(axis) == owner, block, jnp.zeros_like(block))
    return lax.psum(block, axis)


def forward_product(matrix, vector):
    return jnp.einsum("nij,njk->nik", matrix, vector, precision=lax.Precision.HIGHEST)


def transpose_product(matrix, vector):
    return jnp.einsum("nij,nik->njk", matrix, vector, precision=lax.Precision.HIGHEST)


def column_panel(vector):
    group_ratio = lax.axis_size("pcol") // lax.axis_size("prow")
    col_index = lax.axis_index("pcol")
    received = broadcast(vector, "prow", col_index // group_ratio)
    col_width = vector.shape[1] // group_ratio
    return lax.dynamic_slice_in_dim(received, col_index % group_ratio * col_width, col_width, 1)


def column_total(partial_value):
    return lax.psum(partial_value, "pcol")


def regroup(column_rows):
    group_ratio = lax.axis_size("pcol") // lax.axis_size("prow")
    row_index = lax.axis_index("prow")
    col_width = column_rows.shape[1]
    complete = lax.all_gather(column_rows, "pcol", axis=1, tiled=True)
    return lax.dynamic_slice_in_dim(
        complete, row_index * (col_width * group_ratio), col_width * group_ratio, 1
    )


def row_total(partial_value):
    return regroup(lax.psum(partial_value, "prow"))


def local_mask(tile_mask, rows_here, cols_here):
    row_tiles = (lax.axis_index("prow") * rows_here + lax.iota(jnp.int32, rows_here)) // TILE
    col_tiles = (lax.axis_index("pcol") * cols_here + lax.iota(jnp.int32, cols_here)) // TILE
    table = jnp.take(tile_mask[0], row_tiles, axis=1)
    table = jnp.take(table, col_tiles, axis=2)
    return table.astype(jnp.float32)


def per_device_any(diag_inverse, root_inverse, coupling, tile_mask, sketch, root_sketch):
    layer_inverse = diag_inverse[0]
    rows_here = coupling.shape[2]
    cols_here = coupling.shape[3]
    blocks = coupling[0] * local_mask(tile_mask, rows_here, cols_here)
    rhs_local = sketch[0]
    leaves = column_total(forward_product(layer_inverse[0:2], column_panel(rhs_local[0:2])))
    fed_leaves = column_panel(leaves)
    mid_part = forward_product(blocks[0:2], fed_leaves)
    root_part = forward_product(blocks[2:4], fed_leaves)
    mid_rhs = rhs_local[2] - column_total(mid_part[0] + mid_part[1])
    middle = column_total(forward_product(layer_inverse[2:3], column_panel(mid_rhs[None])))[0]
    upper_part = forward_product(blocks[4:5], column_panel(middle[None]))[0]
    update = lax.psum(root_part[0] + root_part[1] + upper_part, ("layer", "pcol"))
    root_forward = column_total(
        forward_product(root_inverse[None], column_panel((root_sketch - update)[None]))
    )[0]
    root_solution = row_total(transpose_product(root_inverse[None], root_forward[None]))[0]
    spread_root = jnp.broadcast_to(root_solution, (3,) + root_solution.shape)
    back_terms = row_total(transpose_product(blocks[2:5], spread_root))
    mid_back = middle - back_terms[2]
    mid_solution = row_total(transpose_product(layer_inverse[2:3], mid_back[None]))[0]
    spread_mid = jnp.broadcast_to(mid_solution, (2,) + mid_solution.shape)
    leaf_terms = row_total(transpose_product(blocks[0:2], spread_mid))
    leaf_back = leaves - leaf_terms - back_terms[0:2]
    leaf_solution = row_total(transpose_product(layer_inverse[0:2], leaf_back))
    solution = jnp.concatenate([leaf_solution, mid_solution[None]], axis=0)[None]
    return (solution, root_solution)

GRID = ("prow", "pcol")
SIDE = 4


def dot(matrices, vectors):
    return jnp.einsum("nij,njk->nik", matrices, vectors, precision=lax.Precision.HIGH)


def dot_t(matrices, vectors):
    return jnp.einsum("nij,nik->njk", matrices, vectors, precision=lax.Precision.HIGH)


def send(value, target):
    pairs = []
    for i in range(SIDE):
        for j in range(SIDE):
            a, b = target(i, j)
            if (a, b) != (i, j):
                pairs.append((i * SIDE + j, a * SIDE + b))
    return lax.ppermute(value, GRID, pairs)


def after(value, earlier):
    return lax.optimization_barrier((value, earlier))[0]


def swap_layers(value):
    return lax.ppermute(value, "layer", [(0, 1), (1, 0)])


def pick(values, index):
    low = jnp.where(index % 2 == 0, values[0], values[1])
    high = jnp.where(index % 2 == 0, values[2], values[3])
    return jnp.where(index // 2 == 0, low, high)


def per_device_square(diag_inverse, root_inverse, coupling, tile_mask, sketch, root_sketch):
    i, j = lax.axis_index("prow"), lax.axis_index("pcol")
    layer = lax.axis_index("layer")
    rows_here, cols_here = root_inverse.shape
    size = rows_here // SIDE
    half = sketch.shape[3] // 2

    def chunk(value, index):
        return lax.dynamic_slice_in_dim(value, index * size, size, value.ndim - 2)

    def natural(parts, turn):
        return jnp.concatenate([pick(parts, turn ^ k) for k in range(SIDE)], axis=1)

    def reduce_rows(partial):
        moved = [send(chunk(partial, j ^ k), lambda a, b: (a, b ^ k)) for k in (3, 2, 1)]
        return chunk(partial, j) + moved[0] + moved[1] + moved[2]

    def gather_rows(value):
        parts = [send(value, lambda a, b: (a, b ^ k)) for k in range(1, SIDE)]
        return natural([value] + parts, j)

    def gather_columns(value):
        parts = [send(value, lambda a, b: (b ^ k, a)) for k in range(SIDE)]
        parts[0] = jnp.where(i == j, value, parts[0])
        return natural(parts, i)

    def reduce_columns(partial):
        near = [chunk(partial, j)] + [
            send(chunk(partial, j ^ k), lambda a, b: (a, b ^ k)) for k in range(1, SIDE)
        ]
        parts = [pick(near, i ^ j ^ k) for k in range(SIDE)]
        moved = [send(parts[k], lambda a, b: (a ^ k, b)) for k in (2, 3, 1)]
        return parts[0] + moved[0] + moved[1] + moved[2]

    def columns(value, which):
        return lax.dynamic_slice_in_dim(value, which * half, half, value.ndim - 1)

    row_tiles = (i * rows_here + lax.iota(jnp.int32, rows_here)) // TILE
    col_tiles = (j * cols_here + lax.iota(jnp.int32, cols_here)) // TILE
    tiles = lax.iota(jnp.int32, tile_mask.shape[2])
    row_pick = (row_tiles[:, None] == tiles[None]).astype(jnp.float32)
    col_pick = (tiles[:, None] == col_tiles[None]).astype(jnp.float32)

    def blocks(first, last):
        rows = jnp.einsum("rt,ntu->nru", row_pick, tile_mask[0, first:last].astype(jnp.float32))
        return coupling[0, first:last] * jnp.einsum("nru,uc->nrc", rows, col_pick)

    rhs = chunk(sketch[0], j)
    root_rhs = chunk(root_sketch, j)

    lower = diag_inverse[0, 0:2]
    first = gather_columns(rhs[0:2])
    leaves, fed = [], []
    for a in range(2):
        leaves.append(reduce_rows(dot(lower[a : a + 1], first[a : a + 1])))
        fed.append(gather_columns(leaves[a]))
    to_mid, to_root, mid_root = blocks(0, 2), blocks(2, 4), blocks(4, 5)
    upper = diag_inverse[0, 2:3]
    root = root_inverse[None]
    mid_part = dot(to_mid[0:1], fed[0]) + dot(to_mid[1:2], fed[1])
    mid_rhs = rhs[2:3] - reduce_rows(mid_part)
    root_part = dot(to_root[0:1], fed[0]) + dot(to_root[1:2], fed[1])
    middle = reduce_rows(dot(upper, gather_columns(mid_rhs)))
    root_part = root_part + dot(mid_root, gather_columns(middle))

    mine = columns(root_part, layer) + swap_layers(columns(root_part, 1 - layer))
    root_in = columns(root_rhs, layer)[None] - reduce_rows(mine)
    root_forward = dot(root, gather_columns(root_in))
    root_forward = root_forward + send(root_forward, lambda a, b: (a, b ^ 1))
    root_forward = root_forward + send(root_forward, lambda a, b: (a, b ^ 2))
    root_half = gather_rows(reduce_columns(dot_t(root, root_forward)))
    other_half = swap_layers(root_half)
    first = layer == 0
    root_rows = jnp.concatenate(
        [jnp.where(first, root_half, other_half), jnp.where(first, other_half, root_half)], axis=2
    )

    def both(value):
        return jnp.broadcast_to(value, (2,) + value.shape[1:])

    mid_back = middle - reduce_columns(dot_t(mid_root, root_rows))
    from_root = dot_t(to_root, both(after(root_rows, mid_back)))
    mid_rows = gather_rows(reduce_columns(dot_t(upper, gather_rows(mid_back))))
    solved = []
    for a in range(2):
        leaf = slice(a, a + 1)
        terms = from_root[leaf] + dot_t(to_mid[leaf], mid_rows)
        leaf_back = leaves[a] - reduce_columns(terms)
        solved.append(gather_rows(reduce_columns(dot_t(lower[leaf], gather_rows(leaf_back)))))
    solved = jnp.concatenate(solved + [mid_rows], axis=0)
    return solved[None], root_rows[0]


def solution(mesh):
    square = dict(mesh.shape) == {"layer": 2, "prow": SIDE, "pcol": SIDE}
    per_device = per_device_square if square else per_device_any
    in_specs = (
        P("layer", None, "prow", "pcol"),
        P("prow", "pcol"),
        P("layer", None, "prow", "pcol"),
        P("layer", None, None, None),
        P("layer", None, "prow", None),
        P("prow", None),
    )
    out_specs = (P("layer", None, "prow", None), P("prow", None))
    return jax.shard_map(
        per_device, mesh=mesh, in_specs=in_specs, out_specs=out_specs, check_vma=False
    )
```
